32 devices in a mesh: path: 16 (over z, x, core), row: 2 (over y).
Axes of the slice: x: 2, y: 2, z: 4, core: 2. Of those that a mesh axis runs over, the one named last changes fastest.
Arguments:
- main_field: bfloat16 [2, 36, 512, 512], P(None, None, 'path', 'row'), may hold values from -6 to 6
- reflect: float32 [9], replicated, may hold values from 0.5 to 1
- curvature: float32 [9], replicated, may hold values from 100 to 1000
- position: float32 [9], replicated, may hold values from 0 to 1
- wave: float32 [4], replicated, may hold values from 0.8 to 1.6
- ghost_pair: int32 [16, 2], replicated, may hold values from 0 to 8, as said below
- ghost_case: int32 [16], replicated, may hold values from 0 to 3, as said below
Outputs:
- glare: float32 [4, 512, 512], P(None, 'path', 'row')
The draws below stay inside these ranges and needn't reach their ends.
Inputs may be any that keep to these rules, and one draw needn't show every extreme that they name: `ghost_pair`: column 0 is the start surface a and column 1 the turning surface b of a ghost path, with b < a; the triples (a, b, ghost_case) of all ghost paths are distinct. `ghost_case`: together with ghost_pair, no triple (start surface, turning surface, case) appears twice.
All inputs are finite; a program needn't handle non-finite values.
Results may differ from the reference program's by a relative error of at most 0.0003.
Values may be sent and summed in bfloat16 or wider, within the bound.
A program may use at most 128 MiB of HBM per device.

```python
import jax
import jax.numpy as jnp
from jax import lax

NG = 512
CASES = 4
SURF = 9
GHOSTS = 16
FIELDS = 36


def ghost_triples(key):
    pair_count = SURF * (SURF - 1) // 2
    total_count = CASES * pair_count
    order = jax.random.permutation(jax.random.fold_in(key, 7), total_count).astype(jnp.int32)
    last_pair = (SURF - 1) * (SURF - 2) // 2
    first_target = (CASES - 1) * pair_count + last_pair
    order = jnp.where(order == first_target, order[0], order)
    order = order.at[0].set(first_target)
    second_target = 0
    order = jnp.where(order == second_target, order[1], order)
    order = order.at[1].set(second_target)
    chosen = order[:GHOSTS]
    rows_list, cols_list = jnp.tril_indices(SURF, -1)
    pair_index = chosen % pair_count
    case_index = chosen // pair_count
    start_surface = rows_list.astype(jnp.int32)[pair_index]
    turn_surface = cols_list.astype(jnp.int32)[pair_index]
    return (start_surface, turn_surface, case_index)


def draw_ghost_pair(key, part):
    start_surface, turn_surface, case_index = ghost_triples(key)
    return jnp.stack([start_surface, turn_surface], 1).astype(jnp.int32)


def draw_ghost_case(key, part):
    start_surface, turn_surface, case_index = ghost_triples(key)
    return case_index.astype(jnp.int32)


def block_scale(own_key, extent, split, low, high):
    gain = 1.0
    for dim, shards_of in split:
        steps = jax.random.uniform(jax.random.fold_in(jax.random.fold_in(own_key, 6), dim), (shards_of,), jnp.float32, low / len(split), high / len(split))
        gain = gain * jnp.repeat(jnp.exp(steps), extent[dim] // shards_of).reshape((-1,) + (1,) * (len(extent) - 1 - dim))
    return gain


def gaussian(stream_key, dims, spread, reach, cuts=(), kind=jnp.bfloat16):
    array = jax.random.normal(stream_key, dims, jnp.float32) * spread
    if len(cuts) > 0:
        array = block_scale(stream_key, dims, cuts, -0.22, 0.18) * array
    return jnp.clip(array, min=-reach, max=reach).astype(kind)


def setup_inputs(seed: int = 0) -> dict:
    seeds = jax.random.split(jax.random.key(seed), 8)
    return {
        "main_field": gaussian(seeds[0], (2, FIELDS, NG, NG), 1.0, 6.0, ((2, 16), (3, 2))),
        "reflect": jnp.clip(jax.random.uniform(seeds[1], (SURF,), jnp.float32, 0.5, 1.0), 0.5, 1.0),
        "curvature": jnp.clip(jax.random.uniform(seeds[2], (SURF,), jnp.float32, 100.0, 1000.0), 100.0, 1000.0),
        "position": jnp.clip(jax.random.uniform(seeds[3], (SURF,), jnp.float32, 0.0, 1.0), 0.0, 1.0),
        "wave": jnp.clip(jax.random.uniform(seeds[4], (CASES,), jnp.float32, 0.8, 1.6), 0.8, 1.6),
        "ghost_pair": draw_ghost_pair(jax.random.fold_in(seeds[7], 71), 0),
        "ghost_case": draw_ghost_case(jax.random.fold_in(seeds[7], 71), 0),
    }


spread_scale = 2000.0


def reference(main_field, reflect, curvature, position, wave, ghost_pair, ghost_case):
    counter = jnp.arange(NG, dtype=jnp.int32)
    shifted = ((counter + NG // 2) % NG - NG // 2).astype(jnp.float32)
    squares = shifted * shifted
    frequency = (squares[:, None] + squares[None, :]) / float(NG * NG)
    centred = (counter - NG // 2).astype(jnp.float32) / float(NG)
    radial = centred[:, None] * centred[:, None] + centred[None, :] * centred[None, :]
    case_ids = jnp.arange(CASES, dtype=jnp.int32)

    def accumulate(total, ghost):
        start_surf = ghost_pair[ghost, 0]
        turn_surf = ghost_pair[ghost, 1]
        case_id = ghost_case[ghost]
        field_id = case_id * SURF + start_surf
        real_part = main_field[0, field_id].astype(jnp.float32)
        imag_part = main_field[1, field_id].astype(jnp.float32)
        start = lax.complex(reflect[start_surf] * real_part, reflect[start_surf] * imag_part)
        coefficient = spread_scale * wave[case_id] * (position[start_surf] - position[turn_surf])
        phase = coefficient * frequency
        transfer = lax.complex(jnp.cos(phase), -jnp.sin(phase))
        first_hop = jnp.fft.ifft2(transfer * jnp.fft.fft2(start))
        screen = curvature[turn_surf] * radial
        turned = lax.complex(reflect[turn_surf] * jnp.cos(screen), reflect[turn_surf] * jnp.sin(screen)) * first_hop
        second_hop = jnp.fft.ifft2(transfer * jnp.fft.fft2(turned))
        intensity = jnp.real(second_hop) ** 2 + jnp.imag(second_hop) ** 2
        one_hot = (case_ids == case_id).astype(jnp.float32)
        return total + one_hot[:, None, None] * intensity[None], None

    initial = jnp.zeros((CASES, NG, NG), jnp.float32)
    total, _ = lax.scan(accumulate, initial, jnp.arange(GHOSTS, dtype=jnp.int32))
    return total * (CASES / GHOSTS)
```

```python
import functools

import jax
import jax.numpy as jnp
import numpy as np
from jax import lax
from jax.experimental import pallas as pl
from jax.experimental.pallas import tpu as pltpu
from jax.sharding import PartitionSpec as P

CASES = 4
SURF = 9

spread_scale = 2000.0

BF16 = jnp.bfloat16
F32 = jnp.float32
MESH = pl.DeviceIdType.MESH
SMEM = pl.BlockSpec(memory_space=pltpu.SMEM)
VMEM = pl.BlockSpec(memory_space=pltpu.VMEM)

TURN = 2.0 * np.pi
TURN_1 = float(np.float32(6.28125))
TURN_2 = float(np.float32(TURN - 6.28125))


def halves(values):
    high = values.astype(BF16)
    return high, (values - high.astype(F32)).astype(BF16)


def cosine_table(cells):
    counter = np.arange(cells, dtype=np.int64)
    exact = np.cos(TURN / cells * (counter[:, None] * counter[None, :] % cells)) / cells
    high = exact.astype(np.float32).astype(jnp.bfloat16)
    low = (exact - high.astype(np.float64)).astype(np.float32).astype(jnp.bfloat16)
    return np.stack([high, low])


def dot(left, right):
    return jnp.dot(left, right, preferred_element_type=F32)


def dot3(left_high, left_low, right_high, right_low):
    return dot(left_high, right_high) + dot(left_high, right_low) + dot(left_low, right_high)


def cos_sin(phase):
    turns = jnp.floor(phase * (1.0 / TURN) + 0.5)
    rest = (phase - turns * TURN_1) - turns * TURN_2
    return jnp.cos(rest), jnp.sin(rest)


def ghost_scalars(reflect, curvature, position, wave, pair, case, ghost):
    start, turn = pair[ghost, 0], pair[ghost, 1]
    coefficient = spread_scale * wave[case[ghost]] * (position[start] - position[turn])
    return coefficient, curvature[turn], reflect[start] * reflect[turn]


def build_operator(cells, coefficient, power, table, spread, screened, both):
    counter = lax.broadcasted_iota(jnp.int32, (16, cells), 1)
    row = lax.broadcasted_iota(jnp.int32, (16, cells), 0)
    shifted = ((counter + cells // 2) % cells - cells // 2).astype(F32)
    cosine, sine = cos_sin(coefficient * (shifted * shifted / float(cells * cells)))
    transfer = jnp.where(row == 0, cosine, jnp.where(row == 1, -sine, 0.0))
    high, low = halves(transfer)
    kernel_rows = dot3(high, low, table[0], table[1])
    centred = (counter - cells // 2).astype(F32) / float(cells)
    screen_cos, screen_sin = cos_sin(power * (centred * centred))
    screen_cos, screen_sin = screen_cos[0:1], screen_sin[0:1]
    step = 128
    for begin in range(0, cells, step):
        rows = pl.ds(begin, step)
        real, imag = (
            pltpu.roll(
                jnp.broadcast_to(kernel_rows[part : part + 1], (step, cells)),
                begin, 1, stride=1, stride_axis=0,
            )
            for part in (0, 1)
        )
        spread[0, rows, :], spread[1, rows, :] = halves(real)
        spread[2, rows, :], spread[3, rows, :] = halves(imag)
        screened[0, rows, :], screened[1, rows, :] = halves(real * screen_cos - imag * screen_sin)
        screened[2, rows, :], screened[3, rows, :] = halves(real * screen_sin + imag * screen_cos)

    wide = cells // 2

    @pl.loop(0, 2)
    def _(chunk):
        rows = pl.ds(pl.multiple_of(chunk * wide, wide), wide)
        left = [screened[k, rows, :] for k in range(4)]
        right = [spread[k] for k in range(4)]
        real = dot3(left[0], left[1], right[0], right[1]) - dot3(left[2], left[3], right[2], right[3])
        both[0, rows, :], both[1, rows, :] = halves(real)
        imag = dot3(left[0], left[1], right[2], right[3]) + dot3(left[2], left[3], right[0], right[1])
        both[2, rows, :], both[3, rows, :] = halves(imag)


def slab_first(real, imag, slab, both, middle, rows):
    weights = [both[k, :, slab] for k in range(4)]
    new_real = (
        dot(real, weights[0]) + dot(real, weights[1]) - dot(imag, weights[2]) - dot(imag, weights[3])
    )
    middle[0, rows, :], middle[1, rows, :] = halves(new_real)
    new_imag = (
        dot(real, weights[2]) + dot(real, weights[3]) + dot(imag, weights[0]) + dot(imag, weights[1])
    )
    middle[2, rows, :], middle[3, rows, :] = halves(new_imag)


def slab_second(both, middle, rows, power):
    left = [both[k, rows, :] for k in range(4)]
    right = [middle[k] for k in range(4)]
    real = dot3(left[0], left[1], right[0], right[1]) - dot3(left[2], left[3], right[2], right[3])
    imag = dot3(left[0], left[1], right[2], right[3]) + dot3(left[2], left[3], right[0], right[1])
    return power * (real * real + imag * imag)


def scratch_of(cells, slab_cells):
    return [
        pltpu.VMEM((4, cells, cells), BF16),
        pltpu.VMEM((4, cells, cells), BF16),
        pltpu.VMEM((4, cells, cells), BF16),
        pltpu.VMEM((4, cells, slab_cells), BF16),
    ]


def whole_kernel(
    cells, paths, row_count,
    field, table_hbm, reflect, curvature, position, wave, pair, case, out,
    spread, screened, both, middle, table, outgoing, held, bright, got,
    table_sem, send_sem, recv_sem, pass_send, pass_recv, out_send, out_recv,
):
    path, row = lax.axis_index("path"), lax.axis_index("row")
    chip, slab_id = path // row_count, path % row_count
    own = chip * row_count + row
    ghosts = pair.shape[0]
    slab_cells = cells // row_count
    piece = cells // paths
    devices = paths * row_count
    mine = path * row_count + row
    is_home = slab_id == row

    barrier = pltpu.get_barrier_semaphore()

    @pl.loop(1, devices)
    def _(step):
        other = (mine + step) % devices
        pl.semaphore_signal(
            barrier, inc=1, device_id=(other // row_count, other % row_count), device_id_type=MESH
        )

    load_table = pltpu.make_async_copy(table_hbm, table, table_sem)
    load_table.start()

    @pl.loop(0, ghosts)
    def _(ghost):
        index = case[ghost] * SURF + pair[ghost, 0]
        outgoing[ghost, 0] = field[0, index]
        outgoing[ghost, 1] = field[1, index]

    pl.semaphore_wait(barrier, devices - 1)

    def field_copy(ghost):
        return pltpu.make_async_remote_copy(
            src_ref=outgoing.at[ghost],
            dst_ref=held.at[row, path],
            send_sem=send_sem.at[ghost],
            recv_sem=recv_sem.at[path],
            device_id=((ghost // row_count) * row_count + row, ghost % row_count),
            device_id_type=MESH,
        )

    def field_arrival(source):
        return pltpu.make_async_remote_copy(
            src_ref=outgoing.at[0],
            dst_ref=held.at[slab_id, source],
            send_sem=send_sem.at[0],
            recv_sem=recv_sem.at[source],
            device_id=(path, row),
            device_id_type=MESH,
        )

    home_copy = pltpu.make_async_copy(outgoing.at[own], held.at[row, path], recv_sem.at[path])

    @pl.loop(0, ghosts)
    def _(step):
        ghost = (own + ghosts // 2 + step) % ghosts

        @pl.when(jnp.logical_or(ghost != own, jnp.logical_not(is_home)))
        def _():
            field_copy(ghost).start()

    @pl.when(is_home)
    def _():
        home_copy.start()

    load_table.wait()
    coefficient, power, gain = ghost_scalars(
        reflect, curvature, position, wave, pair, case, own
    )
    build_operator(cells, coefficient, power, table, spread, screened, both)

    def pass_copy(source, turn):
        return pltpu.make_async_remote_copy(
            src_ref=held.at[slab_id, source],
            dst_ref=held.at[slab_id, source],
            send_sem=pass_send.at[turn - 1, source],
            recv_sem=pass_recv.at[turn - 1, source],
            device_id=(chip * row_count + (slab_id + turn) % row_count, row),
            device_id_type=MESH,
        )

    def pass_arrival(source, turn):
        return pltpu.make_async_remote_copy(
            src_ref=held.at[slab_id, source],
            dst_ref=held.at[(slab_id + row_count - turn) % row_count, source],
            send_sem=pass_send.at[turn - 1, source],
            recv_sem=pass_recv.at[turn - 1, source],
            device_id=(path, row),
            device_id_type=MESH,
        )

    @pl.loop(0, paths)
    def _(step):
        source = (path + step) % paths

        @pl.when(jnp.logical_or(source != path, jnp.logical_not(is_home)))
        def _():
            field_arrival(source).wait_recv()

        @pl.when(jnp.logical_and(source == path, is_home))
        def _():
            home_copy.wait()

        for turn in range(1, row_count):
            pass_copy(source, turn).start()

    @pl.loop(0, paths)
    def _(source):
        for turn in range(1, row_count):
            pass_arrival(source, turn).wait_recv()

    slab = pl.ds(pl.multiple_of(slab_id * slab_cells, slab_cells), slab_cells)
    parts = 2
    group = paths // parts
    tall = cells // parts

    @pl.loop(0, parts)
    def _(chunk):
        def rows_of(part):
            return jnp.concatenate(
                [
                    held[side, pl.ds(chunk * group, group), part].reshape(tall, slab_cells)
                    for side in range(row_count)
                ],
                axis=1,
            )

        slab_first(
            rows_of(0), rows_of(1), slab, both, middle, pl.ds(pl.multiple_of(chunk * tall, tall), tall)
        )

    def bright_copy(target):
        return pltpu.make_async_remote_copy(
            src_ref=bright.at[target],
            dst_ref=got.at[own],
            send_sem=out_send.at[target],
            recv_sem=out_recv.at[own],
            device_id=(target, slab_id),
            device_id_type=MESH,
        )

    def bright_arrival(ghost):
        return pltpu.make_async_remote_copy(
            src_ref=bright.at[0],
            dst_ref=got.at[ghost],
            send_sem=out_send.at[0],
            recv_sem=out_recv.at[ghost],
            device_id=(path, row),
            device_id_type=MESH,
        )

    home_bright = pltpu.make_async_copy(bright.at[path], got.at[own], out_recv.at[own])

    @pl.loop(0, parts)
    def _(turn):
        chunk = (path // group + 1 + turn) % parts
        rows = pl.ds(pl.multiple_of(chunk * tall, tall), tall)
        intensity = slab_second(both, middle, rows, gain * gain * (CASES / ghosts))
        bright[pl.ds(chunk * group, group)] = intensity.reshape(group, piece, slab_cells)

        @pl.loop(0, group)
        def _(step):
            target = chunk * group + (path + step) % group

            @pl.when(jnp.logical_or(target != path, jnp.logical_not(is_home)))
            def _():
                bright_copy(target).start()

            @pl.when(jnp.logical_and(target == path, is_home))
            def _():
                home_bright.start()

    out[...] = jnp.zeros_like(out)

    @pl.loop(0, ghosts)
    def _(step):
        ghost = (own + step) % ghosts

        @pl.when(jnp.logical_or(ghost != own, jnp.logical_not(is_home)))
        def _():
            bright_arrival(ghost).wait_recv()

        @pl.when(jnp.logical_and(ghost == own, is_home))
        def _():
            home_bright.wait()

        values = got[ghost]
        for index in range(CASES):
            chosen = jnp.where(case[ghost] == index, 1.0, 0.0)
            out[index] += chosen * values

    @pl.loop(0, ghosts)
    def _(ghost):
        @pl.when(jnp.logical_or(ghost != own, jnp.logical_not(is_home)))
        def _():
            field_copy(ghost).wait_send()

    @pl.loop(0, paths)
    def _(source):
        for turn in range(1, row_count):
            pass_copy(source, turn).wait_send()

        @pl.when(jnp.logical_or(source != path, jnp.logical_not(is_home)))
        def _():
            bright_copy(source).wait_send()


def whole(cells, paths, row_count, main_field, table, *small):
    ghosts = small[-1].shape[0]
    piece, slab_cells = cells // paths, cells // row_count
    return pl.pallas_call(
        functools.partial(whole_kernel, cells, paths, row_count),
        out_shape=jax.ShapeDtypeStruct((CASES, piece, slab_cells), F32),
        in_specs=[VMEM, pl.BlockSpec(memory_space=pl.ANY)] + [SMEM] * 6,
        out_specs=VMEM,
        scratch_shapes=scratch_of(cells, slab_cells)
        + [
            pltpu.VMEM((2, cells, cells), BF16),
            pltpu.VMEM((ghosts, 2, piece, slab_cells), BF16),
            pltpu.VMEM((row_count, paths, 2, piece, slab_cells), BF16),
            pltpu.VMEM((paths, piece, slab_cells), F32),
            pltpu.VMEM((ghosts, piece, slab_cells), F32),
            pltpu.SemaphoreType.DMA(()),
            pltpu.SemaphoreType.DMA((ghosts,)),
            pltpu.SemaphoreType.DMA((paths,)),
            pltpu.SemaphoreType.DMA((row_count - 1, paths)),
            pltpu.SemaphoreType.DMA((row_count - 1, paths)),
            pltpu.SemaphoreType.DMA((paths,)),
            pltpu.SemaphoreType.DMA((ghosts,)),
        ],
        compiler_params=pltpu.CompilerParams(
            collective_id=0, has_side_effects=True, vmem_limit_bytes=48 * 1024 * 1024
        ),
    )(main_field, table, *small)


def slab_kernel(
    cells, row_count, field, table, reflect, curvature, position, wave, pair, case, slot, out,
    spread, screened, both, middle,
):
    slab_cells = cells // row_count
    coefficient, power, gain = ghost_scalars(
        reflect, curvature, position, wave, pair, case, slot[0]
    )
    build_operator(cells, coefficient, power, table, spread, screened, both)
    slab = pl.ds(pl.multiple_of(slot[1] * slab_cells, slab_cells), slab_cells)
    tall = cells // 2

    @pl.loop(0, 2)
    def _(chunk):
        rows = pl.ds(pl.multiple_of(chunk * tall, tall), tall)
        slab_first(field[0, rows, :], field[1, rows, :], slab, both, middle, rows)

    @pl.loop(0, 2)
    def _(chunk):
        rows = pl.ds(pl.multiple_of(chunk * tall, tall), tall)
        out[rows, :] = slab_second(both, middle, rows, gain * gain)


def local(main_field, table, *small):
    paths = lax.axis_size("path")
    row_count = lax.axis_size("row")
    piece, slab_cells = main_field.shape[2:]
    cells = piece * paths
    pair, case = small[-2:]
    ghosts = pair.shape[0]
    if piece % 16 == 0 and ghosts == paths and paths % (2 * row_count) == 0 and row_count > 1:
        return whole(cells, paths, row_count, main_field, table, *small)
    per_device = ghosts // paths
    picked = main_field[:, case * SURF + pair[:, 0]]
    picked = picked.reshape(2, paths, per_device, piece, slab_cells)
    arrived = lax.all_to_all(picked, "path", split_axis=1, concat_axis=3, tiled=True)
    fields = lax.all_gather(
        arrived.reshape(2, per_device, cells, slab_cells), "row", axis=3, tiled=True
    )
    bright = []
    for index in range(per_device):
        slot = jnp.stack([lax.axis_index("path") * per_device + index, lax.axis_index("row")])
        bright.append(
            pl.pallas_call(
                functools.partial(slab_kernel, cells, row_count),
                out_shape=jax.ShapeDtypeStruct((cells, slab_cells), F32),
                in_specs=[VMEM, VMEM] + [SMEM] * 7,
                out_specs=VMEM,
                scratch_shapes=scratch_of(cells, slab_cells),
                compiler_params=pltpu.CompilerParams(vmem_limit_bytes=48 * 1024 * 1024),
            )(fields[:, index], table, *small, slot)
        )
    got = lax.all_to_all(jnp.stack(bright), "path", split_axis=1, concat_axis=0, tiled=True)
    got = got.reshape(paths, per_device, piece, slab_cells).reshape(ghosts, piece, slab_cells)
    chosen = (case[:, None] == jnp.arange(CASES, dtype=jnp.int32)).astype(F32)
    total = jnp.sum(chosen[:, :, None, None] * got[:, None], 0)
    return total * (CASES / ghosts)


def solution(mesh):
    in_specs = (P(None, None, "path", "row"), P(), P(), P(), P(), P(), P())
    out_specs = P(None, "path", "row")

    def run(main_field, *small):
        table = cosine_table(main_field.shape[2] * mesh.shape["path"])
        return local(main_field, jnp.asarray(table), *small)

    return jax.shard_map(run, mesh=mesh, in_specs=in_specs, out_specs=out_specs, check_vma=False)
```

```python
import functools

import jax
import jax.numpy as jnp
import numpy as np
from jax import lax
from jax.experimental import pallas as pl
from jax.experimental.pallas import tpu as pltpu
from jax.sharding import PartitionSpec as P

CASES = 4
SURF = 9

spread_scale = 2000.0

BF16 = jnp.bfloat16
F32 = jnp.float32
MESH = pl.DeviceIdType.MESH
SMEM = pl.BlockSpec(memory_space=pltpu.SMEM)
VMEM = pl.BlockSpec(memory_space=pltpu.VMEM)

TURN = 2.0 * np.pi
TURN_1 = float(np.float32(6.28125))
TURN_2 = float(np.float32(TURN - 6.28125))


def halves(values):
    high = values.astype(BF16)
    return high, (values - high.astype(F32)).astype(BF16)


def cosine_table(cells):
    counter = np.arange(cells, dtype=np.int64)
    exact = np.cos(TURN / cells * (counter[:, None] * counter[None, :] % cells)) / cells
    high = exact.astype(np.float32).astype(jnp.bfloat16)
    low = (exact - high.astype(np.float64)).astype(np.float32).astype(jnp.bfloat16)
    return np.stack([high, low])


def dot(left, right):
    return jnp.dot(left, right, preferred_element_type=F32)


def dot3(left_high, left_low, right_high, right_low):
    return dot(left_high, right_high) + dot(left_high, right_low) + dot(left_low, right_high)


def cos_sin(phase):
    turns = jnp.floor(phase * (1.0 / TURN) + 0.5)
    rest = (phase - turns * TURN_1) - turns * TURN_2
    return jnp.cos(rest), jnp.sin(rest)


def ghost_scalars(reflect, curvature, position, wave, pair, case, ghost):
    start, turn = pair[0, ghost], pair[1, ghost]
    coefficient = spread_scale * wave[case[ghost]] * (position[start] - position[turn])
    return coefficient, curvature[turn], reflect[start] * reflect[turn]


def build_operator(cells, coefficient, power, table, spread, screened, both):
    counter = lax.broadcasted_iota(jnp.int32, (16, cells), 1)
    row = lax.broadcasted_iota(jnp.int32, (16, cells), 0)
    shifted = ((counter + cells // 2) % cells - cells // 2).astype(F32)
    cosine, sine = cos_sin(coefficient * (shifted * shifted / float(cells * cells)))
    transfer = jnp.where(row == 0, cosine, jnp.where(row == 1, -sine, 0.0))
    high, low = halves(transfer)
    kernel_rows = dot3(high, low, table[0], table[1])
    centred = (counter - cells // 2).astype(F32) / float(cells)
    screen_cos, screen_sin = cos_sin(power * (centred * centred))
    screen_cos, screen_sin = screen_cos[0:1], screen_sin[0:1]
    step = 128
    for begin in range(0, cells, step):
        rows = pl.ds(begin, step)
        real, imag = (
            pltpu.roll(
                jnp.broadcast_to(kernel_rows[part : part + 1], (step, cells)),
                begin, 1, stride=1, stride_axis=0,
            )
            for part in (0, 1)
        )
        spread[0, rows, :], spread[1, rows, :] = halves(real)
        spread[2, rows, :], spread[3, rows, :] = halves(imag)
        screened[0, rows, :], screened[1, rows, :] = halves(real * screen_cos - imag * screen_sin)
        screened[2, rows, :], screened[3, rows, :] = halves(real * screen_sin + imag * screen_cos)

    wide = cells // 2

    @pl.loop(0, 2)
    def _(chunk):
        rows = pl.ds(pl.multiple_of(chunk * wide, wide), wide)
        left = [screened[k, rows, :] for k in range(4)]
        right = [spread[k] for k in range(4)]
        real = dot3(left[0], left[1], right[0], right[1]) - dot3(left[2], left[3], right[2], right[3])
        both[0, rows, :], both[1, rows, :] = halves(real)
        imag = dot3(left[0], left[1], right[2], right[3]) + dot3(left[2], left[3], right[0], right[1])
        both[2, rows, :], both[3, rows, :] = halves(imag)


def slab_first(real, imag, slab, both, middle, rows):
    weights = [both[k, :, slab] for k in range(4)]
    new_real = (
        dot(real, weights[0]) + dot(real, weights[1]) - dot(imag, weights[2]) - dot(imag, weights[3])
    )
    middle[0, rows, :], middle[1, rows, :] = halves(new_real)
    new_imag = (
        dot(real, weights[2]) + dot(real, weights[3]) + dot(imag, weights[0]) + dot(imag, weights[1])
    )
    middle[2, rows, :], middle[3, rows, :] = halves(new_imag)


def slab_second(both, middle, rows, power):
    left = [both[k, rows, :] for k in range(4)]
    right = [middle[k] for k in range(4)]
    real = dot3(left[0], left[1], right[0], right[1]) - dot3(left[2], left[3], right[2], right[3])
    imag = dot3(left[0], left[1], right[2], right[3]) + dot3(left[2], left[3], right[0], right[1])
    return power * (real * real + imag * imag)


def scratch_of(cells, slab_cells):
    return [
        pltpu.VMEM((4, cells, cells), BF16),
        pltpu.VMEM((4, cells, cells), BF16),
        pltpu.VMEM((4, cells, cells), BF16),
        pltpu.VMEM((4, cells, slab_cells), BF16),
    ]


def whole_kernel(
    cells, paths, row_count,
    field_hbm, table_hbm, *rest,
):
    small_hbm, (out, spread, screened, both, middle, field, table, *small), rest = (
        rest[:6], rest[6:19], rest[19:]
    )
    (
        outgoing, held, bright, got,
        load_sem, send_sem, recv_sem, pass_send, pass_recv, out_send, out_recv,
    ) = rest
    reflect, curvature, position, wave, pair, case = small
    path, row = lax.axis_index("path"), lax.axis_index("row")
    chip, slab_id = path // row_count, path % row_count
    own = chip * row_count + row
    ghosts = case.shape[0]
    slab_cells = cells // row_count
    piece = cells // paths
    devices = paths * row_count
    mine = path * row_count + row
    is_home = slab_id == row

    loads = [
        pltpu.make_async_copy(source, target, load_sem.at[index])
        for index, (source, target) in enumerate(
            zip((field_hbm, table_hbm, *small_hbm), (field, table, *small))
        )
    ]
    for load in loads[2:] + loads[:2]:
        load.start()

    barrier = pltpu.get_barrier_semaphore()

    @pl.loop(1, devices)
    def _(step):
        other = (mine + step) % devices
        pl.semaphore_signal(
            barrier, inc=1, device_id=(other // row_count, other % row_count), device_id_type=MESH
        )

    for load in loads[2:] + loads[:1]:
        load.wait()

    @pl.loop(0, ghosts)
    def _(ghost):
        index = case[ghost] * SURF + pair[0, ghost]
        outgoing[ghost, 0] = field[0, index]
        outgoing[ghost, 1] = field[1, index]

    pl.semaphore_wait(barrier, devices - 1)

    def field_copy(ghost):
        return pltpu.make_async_remote_copy(
            src_ref=outgoing.at[ghost],
            dst_ref=held.at[row, path],
            send_sem=send_sem.at[ghost],
            recv_sem=recv_sem.at[path],
            device_id=((ghost // row_count) * row_count + row, ghost % row_count),
            device_id_type=MESH,
        )

    def field_arrival(source):
        return pltpu.make_async_remote_copy(
            src_ref=outgoing.at[0],
            dst_ref=held.at[slab_id, source],
            send_sem=send_sem.at[0],
            recv_sem=recv_sem.at[source],
            device_id=(path, row),
            device_id_type=MESH,
        )

    home_copy = pltpu.make_async_copy(outgoing.at[own], held.at[row, path], recv_sem.at[path])

    @pl.loop(0, ghosts)
    def _(step):
        ghost = (own + ghosts // 2 + step) % ghosts

        @pl.when(jnp.logical_or(ghost != own, jnp.logical_not(is_home)))
        def _():
            field_copy(ghost).start()

    @pl.when(is_home)
    def _():
        home_copy.start()

    loads[1].wait()
    coefficient, power, gain = ghost_scalars(
        reflect, curvature, position, wave, pair, case, own
    )
    build_operator(cells, coefficient, power, table, spread, screened, both)

    def pass_copy(source, turn):
        return pltpu.make_async_remote_copy(
            src_ref=held.at[slab_id, source],
            dst_ref=held.at[slab_id, source],
            send_sem=pass_send.at[turn - 1, source],
            recv_sem=pass_recv.at[turn - 1, source],
            device_id=(chip * row_count + (slab_id + turn) % row_count, row),
            device_id_type=MESH,
        )

    def pass_arrival(source, turn):
        return pltpu.make_async_remote_copy(
            src_ref=held.at[slab_id, source],
            dst_ref=held.at[(slab_id + row_count - turn) % row_count, source],
            send_sem=pass_send.at[turn - 1, source],
            recv_sem=pass_recv.at[turn - 1, source],
            device_id=(path, row),
            device_id_type=MESH,
        )

    @pl.loop(0, paths)
    def _(step):
        source = (path + step) % paths

        @pl.when(jnp.logical_or(source != path, jnp.logical_not(is_home)))
        def _():
            field_arrival(source).wait_recv()

        @pl.when(jnp.logical_and(source == path, is_home))
        def _():
            home_copy.wait()

        for turn in range(1, row_count):
            pass_copy(source, turn).start()

    @pl.loop(0, paths)
    def _(source):
        for turn in range(1, row_count):
            pass_arrival(source, turn).wait_recv()

    slab = pl.ds(pl.multiple_of(slab_id * slab_cells, slab_cells), slab_cells)
    parts = 2
    group = paths // parts
    tall = cells // parts

    @pl.loop(0, parts)
    def _(chunk):
        def rows_of(part):
            return jnp.concatenate(
                [
                    held[side, pl.ds(chunk * group, group), part].reshape(tall, slab_cells)
                    for side in range(row_count)
                ],
                axis=1,
            )

        slab_first(
            rows_of(0), rows_of(1), slab, both, middle, pl.ds(pl.multiple_of(chunk * tall, tall), tall)
        )

    def bright_copy(target):
        return pltpu.make_async_remote_copy(
            src_ref=bright.at[target],
            dst_ref=got.at[own],
            send_sem=out_send.at[target],
            recv_sem=out_recv.at[own],
            device_id=(target, slab_id),
            device_id_type=MESH,
        )

    def bright_arrival(ghost):
        return pltpu.make_async_remote_copy(
            src_ref=bright.at[0],
            dst_ref=got.at[ghost],
            send_sem=out_send.at[0],
            recv_sem=out_recv.at[ghost],
            device_id=(path, row),
            device_id_type=MESH,
        )

    home_bright = pltpu.make_async_copy(bright.at[path], got.at[own], out_recv.at[own])

    @pl.loop(0, parts)
    def _(turn):
        chunk = (path // group + 1 + turn) % parts
        rows = pl.ds(pl.multiple_of(chunk * tall, tall), tall)
        intensity = slab_second(both, middle, rows, gain * gain * (CASES / ghosts))
        bright[pl.ds(chunk * group, group)] = intensity.reshape(group, piece, slab_cells)

        @pl.loop(0, group)
        def _(step):
            target = chunk * group + (path + step) % group

            @pl.when(jnp.logical_or(target != path, jnp.logical_not(is_home)))
            def _():
                bright_copy(target).start()

            @pl.when(jnp.logical_and(target == path, is_home))
            def _():
                home_bright.start()

    out[...] = jnp.zeros_like(out)

    @pl.loop(0, ghosts)
    def _(step):
        ghost = (own + step) % ghosts

        @pl.when(jnp.logical_or(ghost != own, jnp.logical_not(is_home)))
        def _():
            bright_arrival(ghost).wait_recv()

        @pl.when(jnp.logical_and(ghost == own, is_home))
        def _():
            home_bright.wait()

        values = got[ghost]
        for index in range(CASES):
            chosen = jnp.where(case[ghost] == index, 1.0, 0.0)
            out[index] += chosen * values

    @pl.loop(0, ghosts)
    def _(ghost):
        @pl.when(jnp.logical_or(ghost != own, jnp.logical_not(is_home)))
        def _():
            field_copy(ghost).wait_send()

    @pl.loop(0, paths)
    def _(source):
        for turn in range(1, row_count):
            pass_copy(source, turn).wait_send()

        @pl.when(jnp.logical_or(source != path, jnp.logical_not(is_home)))
        def _():
            bright_copy(source).wait_send()


def whole(cells, paths, row_count, main_field, table, *small):
    ghosts = small[-1].shape[0]
    piece, slab_cells = cells // paths, cells // row_count
    return pl.pallas_call(
        functools.partial(whole_kernel, cells, paths, row_count),
        out_shape=jax.ShapeDtypeStruct((CASES, piece, slab_cells), F32),
        in_specs=[pl.BlockSpec(memory_space=pltpu.HBM)] * 8,
        out_specs=VMEM,
        scratch_shapes=scratch_of(cells, slab_cells)
        + [
            pltpu.VMEM(main_field.shape, BF16),
            pltpu.VMEM((2, cells, cells), BF16),
            *[pltpu.SMEM(array.shape, array.dtype) for array in small],
            pltpu.VMEM((ghosts, 2, piece, slab_cells), BF16),
            pltpu.VMEM((row_count, paths, 2, piece, slab_cells), BF16),
            pltpu.VMEM((paths, piece, slab_cells), F32),
            pltpu.VMEM((ghosts, piece, slab_cells), F32),
            pltpu.SemaphoreType.DMA((8,)),
            pltpu.SemaphoreType.DMA((ghosts,)),
            pltpu.SemaphoreType.DMA((paths,)),
            pltpu.SemaphoreType.DMA((row_count - 1, paths)),
            pltpu.SemaphoreType.DMA((row_count - 1, paths)),
            pltpu.SemaphoreType.DMA((paths,)),
            pltpu.SemaphoreType.DMA((ghosts,)),
        ],
        compiler_params=pltpu.CompilerParams(
            collective_id=0, has_side_effects=True, vmem_limit_bytes=60 * 1024 * 1024
        ),
    )(main_field, table, *small)


def slab_kernel(
    cells, row_count, field, table, reflect, curvature, position, wave, pair, case, slot, out,
    spread, screened, both, middle,
):
    slab_cells = cells // row_count
    coefficient, power, gain = ghost_scalars(
        reflect, curvature, position, wave, pair, case, slot[0]
    )
    build_operator(cells, coefficient, power, table, spread, screened, both)
    slab = pl.ds(pl.multiple_of(slot[1] * slab_cells, slab_cells), slab_cells)
    tall = cells // 2

    @pl.loop(0, 2)
    def _(chunk):
        rows = pl.ds(pl.multiple_of(chunk * tall, tall), tall)
        slab_first(field[0, rows, :], field[1, rows, :], slab, both, middle, rows)

    @pl.loop(0, 2)
    def _(chunk):
        rows = pl.ds(pl.multiple_of(chunk * tall, tall), tall)
        out[rows, :] = slab_second(both, middle, rows, gain * gain)


def local(main_field, table, *small):
    paths = lax.axis_size("path")
    row_count = lax.axis_size("row")
    piece, slab_cells = main_field.shape[2:]
    cells = piece * paths
    pair, case = small[-2:]
    ghosts = case.shape[0]
    if piece % 16 == 0 and ghosts == paths and paths % (2 * row_count) == 0 and row_count > 1:
        return whole(cells, paths, row_count, main_field, table, *small)
    per_device = ghosts // paths
    picked = main_field[:, case * SURF + pair[0]]
    picked = picked.reshape(2, paths, per_device, piece, slab_cells)
    arrived = lax.all_to_all(picked, "path", split_axis=1, concat_axis=3, tiled=True)
    fields = lax.all_gather(
        arrived.reshape(2, per_device, cells, slab_cells), "row", axis=3, tiled=True
    )
    bright = []
    for index in range(per_device):
        slot = jnp.stack([lax.axis_index("path") * per_device + index, lax.axis_index("row")])
        bright.append(
            pl.pallas_call(
                functools.partial(slab_kernel, cells, row_count),
                out_shape=jax.ShapeDtypeStruct((cells, slab_cells), F32),
                in_specs=[VMEM, VMEM] + [SMEM] * 7,
                out_specs=VMEM,
                scratch_shapes=scratch_of(cells, slab_cells),
                compiler_params=pltpu.CompilerParams(vmem_limit_bytes=48 * 1024 * 1024),
            )(fields[:, index], table, *small, slot)
        )
    got = lax.all_to_all(jnp.stack(bright), "path", split_axis=1, concat_axis=0, tiled=True)
    got = got.reshape(paths, per_device, piece, slab_cells).reshape(ghosts, piece, slab_cells)
    chosen = (case[:, None] == jnp.arange(CASES, dtype=jnp.int32)).astype(F32)
    total = jnp.sum(chosen[:, :, None, None] * got[:, None], 0)
    return total * (CASES / ghosts)


def solution(mesh):
    in_specs = (P(None, None, "path", "row"), P(), P(), P(), P(), P(), P())
    out_specs = P(None, "path", "row")

    def run(main_field, reflect, curvature, position, wave, pair, case):
        small = (reflect, curvature, position, wave, pair.T, case)
        table = cosine_table(main_field.shape[2] * mesh.shape["path"])
        return local(main_field, jnp.asarray(table), *small)

    return jax.shard_map(run, mesh=mesh, in_specs=in_specs, out_specs=out_specs, check_vma=False)
```

```python
import functools

import jax
import jax.numpy as jnp
import numpy as np
from jax import lax
from jax.experimental import pallas as pl
from jax.experimental.pallas import tpu as pltpu
from jax.sharding import PartitionSpec as P

CASES = 4
SURF = 9

spread_scale = 2000.0

BF16 = jnp.bfloat16
F32 = jnp.float32
MESH = pl.DeviceIdType.MESH
SMEM = pl.BlockSpec(memory_space=pltpu.SMEM)
VMEM = pl.BlockSpec(memory_space=pltpu.VMEM)

TURN = 2.0 * np.pi
TURN_1 = float(np.float32(6.28125))
TURN_2 = float(np.float32(TURN - 6.28125))


def halves(values):
    high = values.astype(BF16)
    return high, (values - high.astype(F32)).astype(BF16)


def cosine_table(cells):
    counter = np.arange(cells, dtype=np.int64)
    exact = np.cos(TURN / cells * (counter[:, None] * counter[None, :] % cells)) / cells
    high = exact.astype(np.float32).astype(jnp.bfloat16)
    low = (exact - high.astype(np.float64)).astype(np.float32).astype(jnp.bfloat16)
    return np.stack([high, low])


def dot(left, right):
    return jnp.dot(left, right, preferred_element_type=F32)


def dot3(left_high, left_low, right_high, right_low):
    return dot(left_high, right_high) + dot(left_high, right_low) + dot(left_low, right_high)


def cos_sin(phase):
    turns = jnp.floor(phase * (1.0 / TURN) + 0.5)
    rest = (phase - turns * TURN_1) - turns * TURN_2
    return jnp.cos(rest), jnp.sin(rest)


def ghost_scalars(reflect, curvature, position, wave, pair, case, ghost):
    start, turn = pair[0, ghost], pair[1, ghost]
    coefficient = spread_scale * wave[case[ghost]] * (position[start] - position[turn])
    return coefficient, curvature[turn], reflect[start] * reflect[turn]


def build_operator(cells, coefficient, power, table, spread, screened, both):
    counter = lax.broadcasted_iota(jnp.int32, (16, cells), 1)
    row = lax.broadcasted_iota(jnp.int32, (16, cells), 0)
    shifted = ((counter + cells // 2) % cells - cells // 2).astype(F32)
    cosine, sine = cos_sin(coefficient * (shifted * shifted / float(cells * cells)))
    transfer = jnp.where(row == 0, cosine, jnp.where(row == 1, -sine, 0.0))
    high, low = halves(transfer)
    kernel_rows = dot3(high, low, table[0], table[1])
    centred = (counter - cells // 2).astype(F32) / float(cells)
    screen_cos, screen_sin = cos_sin(power * (centred * centred))
    screen_cos, screen_sin = screen_cos[0:1], screen_sin[0:1]
    step = 128
    for begin in range(0, cells, step):
        rows = pl.ds(begin, step)
        real, imag = (
            pltpu.roll(
                jnp.broadcast_to(kernel_rows[part : part + 1], (step, cells)),
                begin, 1, stride=1, stride_axis=0,
            )
            for part in (0, 1)
        )
        spread[0, rows, :], spread[1, rows, :] = halves(real)
        spread[2, rows, :], spread[3, rows, :] = halves(imag)
        screened[0, rows, :], screened[1, rows, :] = halves(real * screen_cos - imag * screen_sin)
        screened[2, rows, :], screened[3, rows, :] = halves(real * screen_sin + imag * screen_cos)

    wide = cells // 2

    @pl.loop(0, 2)
    def _(chunk):
        rows = pl.ds(pl.multiple_of(chunk * wide, wide), wide)
        left = [screened[k, rows, :] for k in range(4)]
        right = [spread[k] for k in range(4)]
        real = dot3(left[0], left[1], right[0], right[1]) - dot3(left[2], left[3], right[2], right[3])
        both[0, rows, :], both[1, rows, :] = halves(real)
        imag = dot3(left[0], left[1], right[2], right[3]) + dot3(left[2], left[3], right[0], right[1])
        both[2, rows, :], both[3, rows, :] = halves(imag)


def slab_first(real, imag, slab, both, middle, rows):
    weights = [both[k, :, slab] for k in range(4)]
    new_real = (
        dot(real, weights[0]) + dot(real, weights[1]) - dot(imag, weights[2]) - dot(imag, weights[3])
    )
    middle[0, rows, :], middle[1, rows, :] = halves(new_real)
    new_imag = (
        dot(real, weights[2]) + dot(real, weights[3]) + dot(imag, weights[0]) + dot(imag, weights[1])
    )
    middle[2, rows, :], middle[3, rows, :] = halves(new_imag)


def slab_second(both, middle, rows, power):
    left = [both[k, rows, :] for k in range(4)]
    right = [middle[k] for k in range(4)]
    real = dot3(left[0], left[1], right[0], right[1]) - dot3(left[2], left[3], right[2], right[3])
    imag = dot3(left[0], left[1], right[2], right[3]) + dot3(left[2], left[3], right[0], right[1])
    return power * (real * real + imag * imag)


def scratch_of(cells, slab_cells):
    return [
        pltpu.VMEM((4, cells, cells), BF16),
        pltpu.VMEM((4, cells, cells), BF16),
        pltpu.VMEM((4, cells, cells), BF16),
        pltpu.VMEM((4, cells, slab_cells), BF16),
    ]


def whole_kernel(
    cells, paths, row_count,
    field_hbm, table_hbm, *rest,
):
    small_hbm, (out, spread, screened, both, middle, field, table, *small), rest = (
        rest[:6], rest[6:19], rest[19:]
    )
    (
        outgoing, held, bright, got,
        load_sem, send_sem, recv_sem, pass_send, pass_recv, out_send, out_recv,
    ) = rest
    reflect, curvature, position, wave, pair, case = small
    path, row = lax.axis_index("path"), lax.axis_index("row")
    chip, slab_id = path // row_count, path % row_count
    own = chip * row_count + row
    ghosts = case.shape[0]
    slab_cells = cells // row_count
    piece = cells // paths
    devices = paths * row_count
    mine = path * row_count + row
    is_home = slab_id == row

    loads = [
        pltpu.make_async_copy(source, target, load_sem.at[index])
        for index, (source, target) in enumerate(
            zip((field_hbm, table_hbm, *small_hbm), (field, table, *small))
        )
    ]
    for load in loads[2:] + loads[:2]:
        load.start()

    barrier = pltpu.get_barrier_semaphore()

    @pl.loop(1, devices)
    def _(step):
        other = (mine + step) % devices
        pl.semaphore_signal(
            barrier, inc=1, device_id=(other // row_count, other % row_count), device_id_type=MESH
        )

    for load in loads[2:] + loads[:1]:
        load.wait()

    @pl.loop(0, ghosts)
    def _(ghost):
        index = case[ghost] * SURF + pair[0, ghost]
        outgoing[ghost, 0] = field[0, index]
        outgoing[ghost, 1] = field[1, index]

    pl.semaphore_wait(barrier, devices - 1)

    def field_copy(ghost):
        return pltpu.make_async_remote_copy(
            src_ref=outgoing.at[ghost],
            dst_ref=held.at[row, path],
            send_sem=send_sem.at[ghost],
            recv_sem=recv_sem.at[path],
            device_id=((ghost // row_count) * row_count + row, ghost % row_count),
            device_id_type=MESH,
        )

    def field_arrival(source):
        return pltpu.make_async_remote_copy(
            src_ref=outgoing.at[0],
            dst_ref=held.at[slab_id, source],
            send_sem=send_sem.at[0],
            recv_sem=recv_sem.at[source],
            device_id=(path, row),
            device_id_type=MESH,
        )

    home_copy = pltpu.make_async_copy(outgoing.at[own], held.at[row, path], recv_sem.at[path])

    @pl.loop(0, ghosts)
    def _(step):
        part = ghosts // 2
        turned = (own + step) % part
        ghost = jnp.where(step >= part, (turned + 3 * (ghosts // 4)) % ghosts, turned + ghosts // 4)

        @pl.when(jnp.logical_or(ghost != own, jnp.logical_not(is_home)))
        def _():
            field_copy(ghost).start()

    @pl.when(is_home)
    def _():
        home_copy.start()

    loads[1].wait()
    coefficient, power, gain = ghost_scalars(
        reflect, curvature, position, wave, pair, case, own
    )
    build_operator(cells, coefficient, power, table, spread, screened, both)

    def pass_copy(source, turn):
        return pltpu.make_async_remote_copy(
            src_ref=held.at[slab_id, source],
            dst_ref=held.at[slab_id, source],
            send_sem=pass_send.at[turn - 1, source],
            recv_sem=pass_recv.at[turn - 1, source],
            device_id=(chip * row_count + (slab_id + turn) % row_count, row),
            device_id_type=MESH,
        )

    def pass_arrival(source, turn):
        return pltpu.make_async_remote_copy(
            src_ref=held.at[slab_id, source],
            dst_ref=held.at[(slab_id + row_count - turn) % row_count, source],
            send_sem=pass_send.at[turn - 1, source],
            recv_sem=pass_recv.at[turn - 1, source],
            device_id=(path, row),
            device_id_type=MESH,
        )

    slab = pl.ds(pl.multiple_of(slab_id * slab_cells, slab_cells), slab_cells)
    parts = 2
    group = paths // parts
    tall = cells // parts

    @pl.loop(0, parts)
    def _(turned):
        chunk = (path // group + turned) % parts

        @pl.loop(0, group)
        def _(step):
            source = chunk * group + (path + step) % group

            @pl.when(jnp.logical_or(source != path, jnp.logical_not(is_home)))
            def _():
                field_arrival(source).wait_recv()

            @pl.when(jnp.logical_and(source == path, is_home))
            def _():
                home_copy.wait()

            for turn in range(1, row_count):
                pass_copy(source, turn).start()

        @pl.loop(0, group)
        def _(step):
            for turn in range(1, row_count):
                pass_arrival(chunk * group + step, turn).wait_recv()

        def rows_of(part):
            return jnp.concatenate(
                [
                    held[side, pl.ds(chunk * group, group), part].reshape(tall, slab_cells)
                    for side in range(row_count)
                ],
                axis=1,
            )

        slab_first(
            rows_of(0), rows_of(1), slab, both, middle, pl.ds(pl.multiple_of(chunk * tall, tall), tall)
        )

    def bright_copy(target):
        return pltpu.make_async_remote_copy(
            src_ref=bright.at[target],
            dst_ref=got.at[own],
            send_sem=out_send.at[target],
            recv_sem=out_recv.at[own],
            device_id=(target, slab_id),
            device_id_type=MESH,
        )

    def bright_arrival(ghost):
        return pltpu.make_async_remote_copy(
            src_ref=bright.at[0],
            dst_ref=got.at[ghost],
            send_sem=out_send.at[0],
            recv_sem=out_recv.at[ghost],
            device_id=(path, row),
            device_id_type=MESH,
        )

    home_bright = pltpu.make_async_copy(bright.at[path], got.at[own], out_recv.at[own])

    @pl.loop(0, parts)
    def _(turn):
        chunk = (path // group + 1 + turn) % parts
        rows = pl.ds(pl.multiple_of(chunk * tall, tall), tall)
        intensity = slab_second(both, middle, rows, gain * gain)
        bright[pl.ds(chunk * group, group)] = intensity.reshape(group, piece, slab_cells)

        @pl.loop(0, group)
        def _(step):
            target = chunk * group + (path + step) % group

            @pl.when(jnp.logical_or(target != path, jnp.logical_not(is_home)))
            def _():
                bright_copy(target).start()

            @pl.when(jnp.logical_and(target == path, is_home))
            def _():
                home_bright.start()

    out[...] = jnp.zeros_like(out)

    @pl.loop(0, ghosts)
    def _(step):
        ghost = (own + step) % ghosts

        @pl.when(jnp.logical_or(ghost != own, jnp.logical_not(is_home)))
        def _():
            bright_arrival(ghost).wait_recv()

        @pl.when(jnp.logical_and(ghost == own, is_home))
        def _():
            home_bright.wait()

        values = got[ghost]
        for index in range(CASES):
            chosen = jnp.where(case[ghost] == index, 1.0, 0.0)
            out[index] += chosen * values

    @pl.loop(0, ghosts)
    def _(ghost):
        @pl.when(jnp.logical_or(ghost != own, jnp.logical_not(is_home)))
        def _():
            field_copy(ghost).wait_send()

    @pl.loop(0, paths)
    def _(source):
        for turn in range(1, row_count):
            pass_copy(source, turn).wait_send()

        @pl.when(jnp.logical_or(source != path, jnp.logical_not(is_home)))
        def _():
            bright_copy(source).wait_send()


def whole(cells, paths, row_count, main_field, table, *small):
    ghosts = small[-1].shape[0]
    piece, slab_cells = cells // paths, cells // row_count
    return pl.pallas_call(
        functools.partial(whole_kernel, cells, paths, row_count),
        out_shape=jax.ShapeDtypeStruct((CASES, piece, slab_cells), F32),
        in_specs=[pl.BlockSpec(memory_space=pltpu.HBM)] * 8,
        out_specs=VMEM,
        scratch_shapes=scratch_of(cells, slab_cells)
        + [
            pltpu.VMEM(main_field.shape, BF16),
            pltpu.VMEM((2, cells, cells), BF16),
            *[pltpu.SMEM(array.shape, array.dtype) for array in small],
            pltpu.VMEM((ghosts, 2, piece, slab_cells), BF16),
            pltpu.VMEM((row_count, paths, 2, piece, slab_cells), BF16),
            pltpu.VMEM((paths, piece, slab_cells), F32),
            pltpu.VMEM((ghosts, piece, slab_cells), F32),
            pltpu.SemaphoreType.DMA((8,)),
            pltpu.SemaphoreType.DMA((ghosts,)),
            pltpu.SemaphoreType.DMA((paths,)),
            pltpu.SemaphoreType.DMA((row_count - 1, paths)),
            pltpu.SemaphoreType.DMA((row_count - 1, paths)),
            pltpu.SemaphoreType.DMA((paths,)),
            pltpu.SemaphoreType.DMA((ghosts,)),
        ],
        compiler_params=pltpu.CompilerParams(
            collective_id=0, has_side_effects=True, vmem_limit_bytes=60 * 1024 * 1024
        ),
    )(main_field, table, *small)


def slab_kernel(
    cells, row_count, field, table, reflect, curvature, position, wave, pair, case, slot, out,
    spread, screened, both, middle,
):
    slab_cells = cells // row_count
    coefficient, power, gain = ghost_scalars(
        reflect, curvature, position, wave, pair, case, slot[0]
    )
    build_operator(cells, coefficient, power, table, spread, screened, both)
    slab = pl.ds(pl.multiple_of(slot[1] * slab_cells, slab_cells), slab_cells)
    tall = cells // 2

    @pl.loop(0, 2)
    def _(chunk):
        rows = pl.ds(pl.multiple_of(chunk * tall, tall), tall)
        slab_first(field[0, rows, :], field[1, rows, :], slab, both, middle, rows)

    @pl.loop(0, 2)
    def _(chunk):
        rows = pl.ds(pl.multiple_of(chunk * tall, tall), tall)
        out[rows, :] = slab_second(both, middle, rows, gain * gain)


def local(main_field, table, *small):
    paths = lax.axis_size("path")
    row_count = lax.axis_size("row")
    piece, slab_cells = main_field.shape[2:]
    cells = piece * paths
    pair, case = small[-2:]
    ghosts = case.shape[0]
    if piece % 16 == 0 and ghosts == paths and paths % (2 * row_count) == 0 and row_count > 1:
        total = whole(cells, paths, row_count, main_field, table, *small)
        return total * (CASES / ghosts)
    per_device = ghosts // paths
    picked = main_field[:, case * SURF + pair[0]]
    picked = picked.reshape(2, paths, per_device, piece, slab_cells)
    arrived = lax.all_to_all(picked, "path", split_axis=1, concat_axis=3, tiled=True)
    fields = lax.all_gather(
        arrived.reshape(2, per_device, cells, slab_cells), "row", axis=3, tiled=True
    )
    bright = []
    for index in range(per_device):
        slot = jnp.stack([lax.axis_index("path") * per_device + index, lax.axis_index("row")])
        bright.append(
            pl.pallas_call(
                functools.partial(slab_kernel, cells, row_count),
                out_shape=jax.ShapeDtypeStruct((cells, slab_cells), F32),
                in_specs=[VMEM, VMEM] + [SMEM] * 7,
                out_specs=VMEM,
                scratch_shapes=scratch_of(cells, slab_cells),
                compiler_params=pltpu.CompilerParams(vmem_limit_bytes=48 * 1024 * 1024),
            )(fields[:, index], table, *small, slot)
        )
    got = lax.all_to_all(jnp.stack(bright), "path", split_axis=1, concat_axis=0, tiled=True)
    got = got.reshape(paths, per_device, piece, slab_cells).reshape(ghosts, piece, slab_cells)
    chosen = (case[:, None] == jnp.arange(CASES, dtype=jnp.int32)).astype(F32)
    total = jnp.sum(chosen[:, :, None, None] * got[:, None], 0)
    return total * (CASES / ghosts)


def solution(mesh):
    in_specs = (P(None, None, "path", "row"), P(), P(), P(), P(), P(), P())
    out_specs = P(None, "path", "row")

    def run(main_field, reflect, curvature, position, wave, pair, case):
        small = (reflect, curvature, position, wave, pair.T, case)
        table = cosine_table(main_field.shape[2] * mesh.shape["path"])
        return local(main_field, jnp.asarray(table), *small)

    return jax.shard_map(run, mesh=mesh, in_specs=in_specs, out_specs=out_specs, check_vma=False)
```
